32 devices in a mesh: groups: 2 (over y), cls: 4 (over z), img: 4 (over x, core).
Axes of the slice: x: 2, y: 2, z: 4, core: 2. Of those that a mesh axis runs over, the one named last changes fastest.
Arguments:
- particles: bfloat16 [512, 2, 4608], P(('groups', 'img', 'cls')), parts along dimension 0, may hold values from -30 to 30
- classes: bfloat16 [256, 2, 4608], P(('groups', 'cls')), parts along dimension 0, may hold values from -4 to 4
- ctf: float32 [128, 4608], P('groups'), parts along dimension 0, may hold values from 0.1 to 1
- noise_weight: float32 [9216], P('groups'), parts along dimension 0, may hold values from 0.01 to 0.1
- group_ids: int32 [512], P(('groups', 'img', 'cls')), parts along dimension 0, may hold values from 0 to 63
- shifts: int32 [48, 2], P('groups'), parts along dimension 0, may hold values from -6 to 6
Outputs:
- log_resp: float32 [512, 128], P(('groups', 'img'), 'cls'), parts along dimension 0
- averages: float32 [256, 2, 4608], P(('groups', 'cls'), None, 'img'), parts along dimension 0
The draws below stay inside these ranges and needn't reach their ends.
There are 2 independent parts, one for each index of `groups`. The reference program is written for one: setup_inputs(seed, part) draws one part's arguments, and reference() takes and returns one part's arrays. A program takes and returns all parts, laid end to end along the dimension named above; each array names one. Nothing has to cross between parts.
All inputs are finite; a program needn't handle non-finite values.
Results may differ from the reference program's by a relative error of at most 0.012.
The reference program's roundings to bfloat16 on the way (of `templates`, `weighted` and `rho_low`) count: a program that leaves them out, or rounds other values in their place, can miss the bound.
Values may be sent and summed in bfloat16 or wider, within the bound.
A program may use at most 128 MiB of HBM per device.

```python
import math
import jax
import jax.numpy as jnp
from jax import lax

FREQ = 4608
BOX = 128
POSES = 24
GROUPS = 64
CLASSES = 128
PARTICLES = 256


def class_values(key):
    inner = jax.random.fold_in(key, 11)
    values = jnp.clip(jax.random.normal(inner, (CLASSES, 2, FREQ), jnp.float32), -4.0, 4.0)
    return values


def draw_classes(key, part):
    return class_values(key).astype(jnp.bfloat16)


def draw_shifts(key, part):
    return jax.random.randint(jax.random.fold_in(key, 12), (POSES, 2), -6, 7).astype(jnp.int32)


def rotate_rows(values, cos_rows, sin_rows):
    real_part = values[:, 0, :]
    imag_part = values[:, 1, :]
    return jnp.stack([real_part * cos_rows - imag_part * sin_rows, real_part * sin_rows + imag_part * cos_rows], axis=1)


def draw_particles(key, part):
    key_noise = jax.random.fold_in(key, 21)
    key_class = jax.random.fold_in(key, 23)
    key_pose = jax.random.fold_in(key, 24)
    noise = jnp.clip(jax.random.normal(key_noise, (PARTICLES, 2, FREQ), jnp.float32), -4.0, 4.0)
    values = class_values(key).astype(jnp.bfloat16).astype(jnp.float32)
    shifts = draw_shifts(key, part)
    first = jax.random.randint(key_class, (PARTICLES,), 0, CLASSES)
    second = (first + 1) % CLASSES
    pose = jax.random.randint(key_pose, (PARTICLES,), 0, POSES)
    index = jnp.arange(FREQ)
    along_y = (index // BOX).astype(jnp.float32)
    along_x = (index % BOX - BOX // 2).astype(jnp.float32)
    chosen = shifts[pose]
    angle = 2.0 * jnp.pi / BOX * (chosen[:, 0:1].astype(jnp.float32) * along_x[None, :] + chosen[:, 1:2].astype(jnp.float32) * along_y[None, :])
    cos_rows = jnp.cos(angle)
    sin_rows = jnp.sin(angle)
    planted = rotate_rows(values[first], cos_rows, sin_rows) + 0.992 * rotate_rows(values[second], cos_rows, sin_rows)
    rows = jnp.arange(PARTICLES)
    boost = 4608.0 / FREQ
    strength = boost * jnp.where(rows % 3 == 0, 0.9, jnp.where(rows % 3 == 1, 1.3, 1.8))
    chosen_rows = rows % 61 == 7
    result = jnp.where(chosen_rows[:, None, None], strength[:, None, None] * planted, noise)
    return result.astype(jnp.bfloat16)


def with_ends(values, own_key, smallest, top_value):
    extent = values.shape
    index_at = [jax.random.randint(jax.random.fold_in(own_key, axis), (), 0, extent[axis]) for axis in range(len(extent))]
    values = values.at[tuple(index_at)].set(smallest)
    longest = extent.index(max(extent))
    index_at[longest] = (index_at[longest] + 1) % extent[longest]
    return values.at[tuple(index_at)].set(top_value)


def setup_inputs(seed: int = 0, part: int = 0) -> dict:
    splits = jax.random.split(jax.random.key(seed), 7)
    part_splits = jax.random.split(jax.random.fold_in(splits[6], part), 7)
    particles = draw_particles(jax.random.fold_in(jax.random.fold_in(splits[6], part), 71), part)
    classes = draw_classes(jax.random.fold_in(jax.random.fold_in(splits[6], part), 71), part)
    ctf = jnp.clip(jax.random.uniform(part_splits[2], (GROUPS, FREQ), jnp.float32, 0.1, 1.0), 0.1, 1.0)
    noise_weight = jnp.clip(jnp.exp(jax.random.uniform(part_splits[3], (FREQ,), jnp.float32, math.log(0.01), math.log(0.1))), 0.01, 0.1)
    group_ids = with_ends(jax.random.randint(part_splits[4], (PARTICLES,), 0, GROUPS), jax.random.fold_in(part_splits[4], 1), 0, GROUPS - 1).astype(jnp.int32)
    shifts = draw_shifts(jax.random.fold_in(jax.random.fold_in(splits[6], part), 71), part)
    return dict(particles=particles, classes=classes, ctf=ctf, noise_weight=noise_weight, group_ids=group_ids, shifts=shifts)


prior_precision = 0.02


def phase_tables(shifts):
    index = jnp.arange(FREQ)
    along_y = (index // BOX).astype(jnp.float32)
    along_x = (index % BOX - BOX // 2).astype(jnp.float32)
    angle = (2.0 * jnp.pi / BOX) * (shifts[:, 0:1].astype(jnp.float32) * along_x[None, :] + shifts[:, 1:2].astype(jnp.float32) * along_y[None, :])
    return jnp.cos(angle), jnp.sin(angle)


def reference(particles, classes, ctf, noise_weight, group_ids, shifts):
    cos_t, sin_t = phase_tables(shifts)
    real_part = classes[:, 0, :].astype(jnp.float32)
    imag_part = classes[:, 1, :].astype(jnp.float32)
    temp_re = real_part[None] * cos_t[:, None, :] - imag_part[None] * sin_t[:, None, :]
    temp_im = real_part[None] * sin_t[:, None, :] + imag_part[None] * cos_t[:, None, :]
    templates = jnp.stack([temp_re, temp_im], axis=2).astype(jnp.bfloat16)
    templates = templates.reshape(POSES * CLASSES, 2 * FREQ)
    selected = ctf[group_ids]
    weighted = (particles.astype(jnp.float32) * (selected * noise_weight[None, :])[:, None, :]).astype(jnp.bfloat16)
    weighted = weighted.reshape(PARTICLES, 2 * FREQ)
    ctf_weight = ctf * ctf * noise_weight[None, :]
    power = jnp.dot(ctf_weight, (real_part * real_part + imag_part * imag_part).T, precision=lax.Precision.HIGHEST)
    penalty = power[group_ids]
    cross = jnp.dot(weighted.astype(jnp.float32), templates.astype(jnp.float32).T, precision=lax.Precision.HIGHEST)
    scores = cross.reshape(PARTICLES, POSES, CLASSES) - 0.5 * penalty[:, None, :]
    peak = jnp.max(scores, axis=(1, 2))
    log_norm = peak + jnp.log(jnp.sum(jnp.exp(scores - peak[:, None, None]), axis=(1, 2)))
    pose_peak = jnp.max(scores, axis=1)
    log_resp = pose_peak + jnp.log(jnp.sum(jnp.exp(scores - pose_peak[:, None, :]), axis=1)) - log_norm[:, None]
    rho = jnp.exp(scores - log_norm[:, None, None])
    rho_low = rho.astype(jnp.bfloat16).reshape(PARTICLES, POSES * CLASSES)
    sums = jnp.dot(rho_low.astype(jnp.float32).T, weighted.astype(jnp.float32), precision=lax.Precision.HIGHEST)
    sums = sums.reshape(POSES, CLASSES, 2, FREQ)
    cos_b = cos_t[:, None, :]
    sin_b = sin_t[:, None, :]
    numer_re = jnp.sum(sums[:, :, 0, :] * cos_b + sums[:, :, 1, :] * sin_b, axis=0)
    numer_im = jnp.sum(sums[:, :, 1, :] * cos_b - sums[:, :, 0, :] * sin_b, axis=0)
    numer = jnp.stack([numer_re, numer_im], axis=1)
    onehot = (group_ids[:, None] == jnp.arange(GROUPS)[None, :]).astype(jnp.float32)
    pose_total = jnp.sum(rho, axis=1)
    mass = jnp.dot(pose_total.T, onehot, precision=lax.Precision.HIGHEST)
    denom = jnp.dot(mass, ctf_weight, precision=lax.Precision.HIGHEST)
    averages = numer / (denom[:, None, :] + prior_precision)
    return log_resp, averages
```

```python
import functools

import jax
import jax.numpy as jnp
from jax import lax
from jax.experimental import pallas as pl
from jax.experimental.pallas import tpu as pltpu
from jax.sharding import PartitionSpec as P

BOX = 128
LANES = 128
MESH = pl.DeviceIdType.MESH
HIGHEST = lax.Precision.HIGHEST
NT = (((1,), (1,)), ((), ()))

prior_precision = 0.02


def phase_tables(shifts, freq):
    step = 2.0 * jnp.pi / BOX
    along_y = jnp.arange(freq // BOX).astype(jnp.float32)
    along_x = (jnp.arange(BOX) - BOX // 2).astype(jnp.float32)
    angle_x = step * (shifts[:, 0:1].astype(jnp.float32) * along_x[None, :])
    angle_y = step * (shifts[:, 1:2].astype(jnp.float32) * along_y[None, :])
    cos_x, sin_x = jnp.cos(angle_x)[:, None, :], jnp.sin(angle_x)[:, None, :]
    cos_y, sin_y = jnp.cos(angle_y)[:, :, None], jnp.sin(angle_y)[:, :, None]
    shape = (shifts.shape[0], freq)
    return (
        (cos_x * cos_y - sin_x * sin_y).reshape(shape),
        (sin_x * cos_y + cos_x * sin_y).reshape(shape),
    )


def kernel(
    n_cls, n_img, chunk,
    ids_s, ids_v, part_ref, cls_ref, ctf_ref, nw_ref, cos_ref, sin_ref,
    resp_ref, avg_ref,
    wbuf, sel, temps, scores, rho_low, stat, mass_buf, send_buf, recv_buf, own,
    gs_sem, gr_sem, ss_sem, sr_sem, ms_sem, mr_sem, ns_sem, nr_sem,
):
    rows = part_ref.shape[0]
    freq = ctf_ref.shape[1]
    groups = ctf_ref.shape[0]
    classes = cls_ref.shape[0]
    poses = cos_ref.shape[0]
    total = rows * n_cls
    part_freq = freq // n_img
    my_cls = lax.axis_index("cls")
    my_img = lax.axis_index("img")

    barrier = pltpu.get_barrier_semaphore()
    for d in range(1, n_cls):
        pl.semaphore_signal(
            barrier, inc=1, device_id={"cls": lax.rem(my_cls + d, n_cls)}, device_id_type=MESH
        )
    for d in range(1, n_img):
        pl.semaphore_signal(
            barrier, inc=1, device_id={"img": lax.rem(my_img + d, n_img)}, device_id_type=MESH
        )

    for i in range(rows):
        sel[pl.ds(i, 1), :] = ctf_ref[pl.ds(ids_s[i], 1), :] * nw_ref[...]
    for part in range(2):
        cols = slice(part * freq, (part + 1) * freq)
        wbuf[my_cls, :, cols] = (
            part_ref[:, cols].astype(jnp.float32) * sel[...]
        ).astype(jnp.bfloat16)
    pad_groups = wbuf.shape[2] - 2 * freq
    wbuf[my_cls, :, 2 * freq :] = (
        ids_v[...] == lax.broadcasted_iota(jnp.int32, (rows, pad_groups), 1)
    ).astype(jnp.float32).astype(jnp.bfloat16)

    pl.semaphore_wait(barrier, n_cls + n_img - 2)

    def gather_copy(d, slot):
        return pltpu.make_async_remote_copy(
            src_ref=wbuf.at[slot],
            dst_ref=wbuf.at[slot],
            send_sem=gs_sem.at[d],
            recv_sem=gr_sem.at[d],
            device_id={"cls": lax.rem(my_cls + d, n_cls)},
            device_id_type=MESH,
        )

    for d in range(1, n_cls):
        gather_copy(d, my_cls).start()

    def build(c, power):
        at = pl.multiple_of(c * chunk, LANES)
        at_im = pl.multiple_of(freq + c * chunk, LANES)
        re = cls_ref[:, pl.ds(at, chunk)].astype(jnp.float32)
        im = cls_ref[:, pl.ds(at_im, chunk)].astype(jnp.float32)
        for r in range(poses):
            cos_r = cos_ref[r : r + 1, pl.ds(at, chunk)]
            sin_r = sin_ref[r : r + 1, pl.ds(at, chunk)]
            out = slice(r * classes, (r + 1) * classes)
            temps[out, pl.ds(at, chunk)] = (re * cos_r - im * sin_r).astype(jnp.bfloat16)
            temps[out, pl.ds(at_im, chunk)] = (re * sin_r + im * cos_r).astype(jnp.bfloat16)
        ctf = ctf_ref[:, pl.ds(at, chunk)]
        weight = ctf * ctf * nw_ref[:, pl.ds(at, chunk)]
        return power + lax.dot_general(
            re * re + im * im, weight, NT, precision=HIGHEST,
            preferred_element_type=jnp.float32,
        )

    power = lax.fori_loop(
        0, freq // chunk, build, jnp.zeros((classes, groups), jnp.float32)
    )

    for d in range(1, n_cls):
        gather_copy(d, lax.rem(my_cls + n_cls - d, n_cls)).wait_recv()

    marks = wbuf[:, :, 2 * freq :].reshape(total, pad_groups)[:, :groups].astype(jnp.float32)
    penalty = lax.dot_general(
        power, marks, NT, precision=HIGHEST, preferred_element_type=jnp.float32
    )
    scores[...] = jnp.zeros_like(scores)

    def cross(c, carry):
        at = pl.multiple_of(c * 2 * chunk, LANES)
        scores[...] += lax.dot_general(
            temps[:, pl.ds(at, 2 * chunk)],
            wbuf[:, :, pl.ds(at, 2 * chunk)].reshape(total, 2 * chunk),
            NT,
            preferred_element_type=jnp.float32,
        )
        return carry

    lax.fori_loop(0, freq // chunk, cross, 0)

    value = scores[...].reshape(poses, classes, total) - 0.5 * penalty[None]
    pose_peak = jnp.max(value, axis=0)
    pose_sum = jnp.sum(jnp.exp(value - pose_peak[None]), axis=0)
    peak = jnp.max(pose_peak, axis=0, keepdims=True)
    stat[0, 0:1, :total] = peak
    stat[0, 1:2, :total] = jnp.sum(
        pose_sum * jnp.exp(pose_peak - peak), axis=0, keepdims=True
    )

    def stat_copy(d):
        return pltpu.make_async_remote_copy(
            src_ref=stat.at[0],
            dst_ref=stat.at[d],
            send_sem=ss_sem.at[d],
            recv_sem=sr_sem.at[d],
            device_id={"cls": lax.rem(my_cls + d, n_cls)},
            device_id_type=MESH,
        )

    for d in range(1, n_cls):
        stat_copy(d).start()
    for d in range(1, n_cls):
        stat_copy(d).wait_recv()
    whole_peak = peak
    for d in range(1, n_cls):
        whole_peak = jnp.maximum(whole_peak, stat[d, 0:1, :total])
    norm = jnp.zeros_like(peak)
    for d in range(n_cls):
        norm += stat[d, 1:2, :total] * jnp.exp(stat[d, 0:1, :total] - whole_peak)
    log_norm = whole_peak + jnp.log(norm)
    resp_ref[...] = pose_peak + jnp.log(pose_sum) - log_norm
    rho = jnp.exp(value - log_norm[None])
    rho_low[...] = rho.reshape(poses * classes, total).astype(jnp.bfloat16)
    mass_buf[0] = jnp.dot(
        jnp.sum(rho, axis=0),
        wbuf[:, :, 2 * freq :].reshape(total, pad_groups).astype(jnp.float32),
        precision=HIGHEST,
        preferred_element_type=jnp.float32,
    )

    def to_img(src, dst, d, send, recv):
        return pltpu.make_async_remote_copy(
            src_ref=src.at[d] if src is send_buf else src.at[0],
            dst_ref=dst.at[d],
            send_sem=send.at[d],
            recv_sem=recv.at[d],
            device_id={"img": lax.rem(my_img + d, n_img)},
            device_id_type=MESH,
        )

    for d in range(1, n_img):
        to_img(mass_buf, mass_buf, d, ms_sem, mr_sem).start()

    def numer(target, store):
        def step(c, carry):
            at = pl.multiple_of(target * part_freq + c * chunk, LANES)
            at_im = pl.multiple_of(freq + target * part_freq + c * chunk, LANES)
            low = rho_low[...]
            sum_re = jnp.dot(
                low, wbuf[:, :, pl.ds(at, chunk)].reshape(total, chunk),
                preferred_element_type=jnp.float32,
            )
            sum_im = jnp.dot(
                low, wbuf[:, :, pl.ds(at_im, chunk)].reshape(total, chunk),
                preferred_element_type=jnp.float32,
            )
            acc_re = jnp.zeros((classes, chunk), jnp.float32)
            acc_im = jnp.zeros((classes, chunk), jnp.float32)
            for r in range(poses):
                cos_r = cos_ref[r : r + 1, pl.ds(at, chunk)]
                sin_r = sin_ref[r : r + 1, pl.ds(at, chunk)]
                s_re = sum_re[r * classes : (r + 1) * classes]
                s_im = sum_im[r * classes : (r + 1) * classes]
                acc_re += s_re * cos_r + s_im * sin_r
                acc_im += s_im * cos_r - s_re * sin_r
            store(pl.multiple_of(c * chunk, LANES), acc_re, acc_im)
            return carry

        lax.fori_loop(0, part_freq // chunk, step, 0)

    for d in range(1, n_img):
        def store_peer(at, re, im, d=d):
            send_buf[d, :classes, pl.ds(at, chunk)] = re.astype(send_buf.dtype)
            send_buf[d, classes:, pl.ds(at, chunk)] = im.astype(send_buf.dtype)

        numer(lax.rem(my_img + d, n_img), store_peer)
        to_img(send_buf, recv_buf, d, ns_sem, nr_sem).start()

    def store_own(at, re, im):
        own[:classes, pl.ds(at, chunk)] = re
        own[classes:, pl.ds(at, chunk)] = im

    numer(my_img, store_own)

    for d in range(1, n_img):
        to_img(mass_buf, mass_buf, d, ms_sem, mr_sem).wait_recv()
    mass = mass_buf[0]
    for d in range(1, n_img):
        mass += mass_buf[d]
    mine = pl.ds(pl.multiple_of(my_img * part_freq, LANES), part_freq)
    ctf = ctf_ref[:, mine]
    denom = jnp.dot(
        mass[:, :groups], ctf * ctf * nw_ref[:, mine], precision=HIGHEST,
        preferred_element_type=jnp.float32,
    ) + prior_precision

    for d in range(1, n_img):
        to_img(send_buf, recv_buf, d, ns_sem, nr_sem).wait_recv()
    for part in range(2):
        at = slice(part * classes, (part + 1) * classes)
        value_sum = own[at]
        for d in range(1, n_img):
            value_sum += recv_buf[d, at].astype(jnp.float32)
        avg_ref[part] = value_sum / denom

    for d in range(1, n_cls):
        gather_copy(d, my_cls).wait_send()
        stat_copy(d).wait_send()
    for d in range(1, n_img):
        to_img(mass_buf, mass_buf, d, ms_sem, mr_sem).wait_send()
        to_img(send_buf, recv_buf, d, ns_sem, nr_sem).wait_send()


def local(n_cls, n_img, particles, classes, ctf, noise_weight, group_ids, shifts):
    rows, _, freq = particles.shape
    cls_rows = classes.shape[0]
    poses = shifts.shape[0]
    groups = ctf.shape[0]
    total = rows * n_cls
    part_freq = freq // n_img
    chunk = 384 if part_freq % 384 == 0 else LANES
    pad_groups = -(-groups // LANES) * LANES
    pad_total = -(-total // LANES) * LANES
    cos_t, sin_t = phase_tables(shifts, freq)
    vmem = pl.BlockSpec(memory_space=pltpu.VMEM)
    dma = pltpu.SemaphoreType.DMA
    resp, avg = pl.pallas_call(
        functools.partial(kernel, n_cls, n_img, chunk),
        out_shape=(
            jax.ShapeDtypeStruct((cls_rows, total), jnp.float32),
            jax.ShapeDtypeStruct((2, cls_rows, part_freq), jnp.float32),
        ),
        in_specs=[pl.BlockSpec(memory_space=pltpu.SMEM)] + [vmem] * 7,
        out_specs=(vmem, vmem),
        scratch_shapes=[
            pltpu.VMEM((n_cls, rows, 2 * freq + pad_groups), jnp.bfloat16),
            pltpu.VMEM((rows, freq), jnp.float32),
            pltpu.VMEM((poses * cls_rows, 2 * freq), jnp.bfloat16),
            pltpu.VMEM((poses * cls_rows, total), jnp.float32),
            pltpu.VMEM((poses * cls_rows, total), jnp.bfloat16),
            pltpu.VMEM((n_cls, 8, pad_total), jnp.float32),
            pltpu.VMEM((n_img, cls_rows, pad_groups), jnp.float32),
            pltpu.VMEM((n_img, 2 * cls_rows, part_freq), jnp.bfloat16),
            pltpu.VMEM((n_img, 2 * cls_rows, part_freq), jnp.bfloat16),
            pltpu.VMEM((2 * cls_rows, part_freq), jnp.float32),
            dma((n_cls,)), dma((n_cls,)), dma((n_cls,)), dma((n_cls,)),
            dma((n_img,)), dma((n_img,)), dma((n_img,)), dma((n_img,)),
        ],
        compiler_params=pltpu.CompilerParams(
            collective_id=0, has_side_effects=True, vmem_limit_bytes=56 << 20
        ),
    )(
        group_ids,
        group_ids[:, None],
        particles.reshape(rows, 2 * freq),
        classes.reshape(cls_rows, 2 * freq),
        ctf,
        noise_weight[None, :],
        cos_t,
        sin_t,
    )
    return resp.T, avg.transpose(1, 0, 2)


def solution(mesh):
    placed = (
        P(("groups", "img", "cls"), None, None),
        P(("groups", "cls"), None, None),
        P("groups", None),
        P("groups"),
        P(("groups", "img", "cls")),
        P("groups", None),
    )
    return jax.shard_map(
        functools.partial(local, mesh.shape["cls"], mesh.shape["img"]),
        mesh=mesh,
        in_specs=placed,
        out_specs=(P(("groups", "img"), "cls"), P(("groups", "cls"), None, "img")),
        check_vma=False,
    )
```

```python
import functools

import jax
import jax.numpy as jnp
from jax import lax
from jax.experimental import pallas as pl
from jax.experimental.pallas import tpu as pltpu
from jax.sharding import PartitionSpec as P

BOX = 128
LANES = 128
MESH = pl.DeviceIdType.MESH
HIGHEST = lax.Precision.HIGHEST
NT = (((1,), (1,)), ((), ()))

prior_precision = 0.02


def fill_phase_tables(shifts, cos_ref, sin_ref):
    poses, freq = cos_ref.shape
    step = 2.0 * jnp.pi / BOX
    lane = lax.broadcasted_iota(jnp.int32, (poses, BOX), 1)
    move_x = shifts[:, 0:1].astype(jnp.float32)
    move_y = shifts[:, 1:2].astype(jnp.float32)
    angle_x = step * (move_x * (lane - BOX // 2).astype(jnp.float32))
    cos_x, sin_x = jnp.cos(angle_x), jnp.sin(angle_x)
    for row in range(freq // BOX):
        if row % BOX == 0:
            angle_y = step * (move_y * (lane + row).astype(jnp.float32))
            cos_rows, sin_rows = jnp.cos(angle_y), jnp.sin(angle_y)
        cos_y = cos_rows[:, row % BOX : row % BOX + 1]
        sin_y = sin_rows[:, row % BOX : row % BOX + 1]
        cols = slice(row * BOX, (row + 1) * BOX)
        cos_ref[:, cols] = cos_x * cos_y - sin_x * sin_y
        sin_ref[:, cols] = sin_x * cos_y + cos_x * sin_y


def kernel(
    n_cls, n_img, chunk, pieces,
    ids_s, part_ref, cls_ref, ctf_ref, nw_ref, shift_ref,
    resp_ref, avg_ref,
    wbuf, sel, onehot, cos_ref, sin_ref, temps, scores, rho_low, stat, mass_buf, send_buf, recv_buf, own,
    right_sem, left_sem, gr_sem, ss_sem, sr_sem, ms_sem, mr_sem, ns_sem, nr_sem,
):
    rows = part_ref.shape[0]
    freq = ctf_ref.shape[1]
    groups = ctf_ref.shape[0]
    classes = cls_ref.shape[0]
    poses = cos_ref.shape[0]
    total = rows * n_cls
    part_freq = freq // n_img
    my_cls = lax.axis_index("cls")
    my_img = lax.axis_index("img")

    barrier = pltpu.get_barrier_semaphore()
    for d in range(1, n_cls):
        pl.semaphore_signal(
            barrier, inc=1, device_id={"cls": lax.rem(my_cls + d, n_cls)}, device_id_type=MESH
        )
    for d in range(1, n_img):
        pl.semaphore_signal(
            barrier, inc=1, device_id={"img": lax.rem(my_img + d, n_img)}, device_id_type=MESH
        )

    for i in range(rows):
        sel[pl.ds(i, 1), :] = ctf_ref[pl.ds(ids_s[i], 1), :] * nw_ref[...]
        onehot[pl.ds(i, 1), :] = (
            lax.broadcasted_iota(jnp.int32, (1, onehot.shape[1]), 1) == ids_s[i]
        ).astype(jnp.float32)
    for part in range(2):
        cols = slice(part * freq, (part + 1) * freq)
        wbuf[my_cls, :, cols] = (
            part_ref[:, cols].astype(jnp.float32) * sel[...]
        ).astype(jnp.bfloat16)
    pad_groups = wbuf.shape[2] - 2 * freq
    wbuf[my_cls, :, 2 * freq :] = onehot[...].astype(jnp.bfloat16)

    pl.semaphore_wait(barrier, n_cls + n_img - 2)

    width = 2 * freq // pieces

    def hop(slot, p, to_right):
        last = pad_groups if p == pieces - 1 else 0
        cols = pl.ds(p * width, width + last)
        return pltpu.make_async_remote_copy(
            src_ref=wbuf.at[slot, :, cols],
            dst_ref=wbuf.at[slot, :, cols],
            send_sem=(right_sem if to_right else left_sem).at[slot, p],
            recv_sem=gr_sem.at[slot, p],
            device_id={"cls": my_cls + 1 if to_right else my_cls - 1},
            device_id_type=MESH,
        )

    has_right = my_cls < n_cls - 1
    has_left = my_cls > 0

    def start_right(slot, p):
        @pl.when(has_right)
        def _():
            hop(slot, p, True).start()

    def start_left(slot, p):
        @pl.when(has_left)
        def _():
            hop(slot, p, False).start()

    def relay(h, p):
        @pl.when(my_cls - h >= 0)
        def _():
            hop(my_cls - h, p, False).wait_recv()
            start_right(my_cls - h, p)

        @pl.when(my_cls + h < n_cls)
        def _():
            hop(my_cls + h, p, True).wait_recv()
            start_left(my_cls + h, p)

    for p in range(pieces):
        start_right(my_cls, p)
        start_left(my_cls, p)

    fill_phase_tables(shift_ref[...], cos_ref, sin_ref)

    def build(c, power):
        at = pl.multiple_of(c * chunk, LANES)
        at_im = pl.multiple_of(freq + c * chunk, LANES)
        re = cls_ref[:, pl.ds(at, chunk)].astype(jnp.float32)
        im = cls_ref[:, pl.ds(at_im, chunk)].astype(jnp.float32)
        for r in range(poses):
            cos_r = cos_ref[r : r + 1, pl.ds(at, chunk)]
            sin_r = sin_ref[r : r + 1, pl.ds(at, chunk)]
            out = slice(r * classes, (r + 1) * classes)
            temps[out, pl.ds(at, chunk)] = (re * cos_r - im * sin_r).astype(jnp.bfloat16)
            temps[out, pl.ds(at_im, chunk)] = (re * sin_r + im * cos_r).astype(jnp.bfloat16)
        ctf = ctf_ref[:, pl.ds(at, chunk)]
        weight = ctf * ctf * nw_ref[:, pl.ds(at, chunk)]
        return power + lax.dot_general(
            re * re + im * im, weight, NT, precision=HIGHEST,
            preferred_element_type=jnp.float32,
        )

    power = lax.fori_loop(
        0, freq // chunk, build, jnp.zeros((classes, groups), jnp.float32)
    )

    scores[...] = jnp.zeros_like(scores)

    def relay_all(h, carry):
        for p in range(pieces):
            relay(h, p)
        return carry

    lax.fori_loop(1, n_cls - 1, relay_all, 0)

    steps = width // (2 * chunk)

    def cross(c, carry):
        at = pl.multiple_of(c * 2 * chunk, LANES)
        scores[...] += lax.dot_general(
            temps[:, pl.ds(at, 2 * chunk)],
            wbuf[:, :, pl.ds(at, 2 * chunk)].reshape(total, 2 * chunk),
            NT,
            preferred_element_type=jnp.float32,
        )
        return carry

    for p in range(pieces):
        relay(n_cls - 1, p)
        lax.fori_loop(p * steps, (p + 1) * steps, cross, 0)

    marks = wbuf[:, :, 2 * freq :].reshape(total, pad_groups)[:, :groups].astype(jnp.float32)
    penalty = lax.dot_general(
        power, marks, NT, precision=HIGHEST, preferred_element_type=jnp.float32
    )
    value = scores[...].reshape(poses, classes, total) - 0.5 * penalty[None]
    pose_peak = jnp.max(value, axis=0)
    pose_sum = jnp.sum(jnp.exp(value - pose_peak[None]), axis=0)
    peak = jnp.max(pose_peak, axis=0, keepdims=True)
    stat[0, 0:1, :total] = peak
    stat[0, 1:2, :total] = jnp.sum(
        pose_sum * jnp.exp(pose_peak - peak), axis=0, keepdims=True
    )

    def stat_copy(d):
        return pltpu.make_async_remote_copy(
            src_ref=stat.at[0],
            dst_ref=stat.at[d],
            send_sem=ss_sem.at[d],
            recv_sem=sr_sem.at[d],
            device_id={"cls": lax.rem(my_cls + d, n_cls)},
            device_id_type=MESH,
        )

    for d in range(1, n_cls):
        stat_copy(d).start()
    for d in range(1, n_cls):
        stat_copy(d).wait_recv()
    whole_peak = peak
    for d in range(1, n_cls):
        whole_peak = jnp.maximum(whole_peak, stat[d, 0:1, :total])
    norm = jnp.zeros_like(peak)
    for d in range(n_cls):
        norm += stat[d, 1:2, :total] * jnp.exp(stat[d, 0:1, :total] - whole_peak)
    log_norm = whole_peak + jnp.log(norm)
    resp_ref[...] = pose_peak + jnp.log(pose_sum) - log_norm
    rho = jnp.exp(value - log_norm[None])
    rho_low[...] = rho.reshape(poses * classes, total).astype(jnp.bfloat16)
    mass_buf[0] = jnp.dot(
        jnp.sum(rho, axis=0),
        wbuf[:, :, 2 * freq :].reshape(total, pad_groups).astype(jnp.float32),
        precision=HIGHEST,
        preferred_element_type=jnp.float32,
    )

    def to_img(src, dst, d, send, recv):
        return pltpu.make_async_remote_copy(
            src_ref=src.at[d] if src is send_buf else src.at[0],
            dst_ref=dst.at[d],
            send_sem=send.at[d],
            recv_sem=recv.at[d],
            device_id={"img": lax.rem(my_img + d, n_img)},
            device_id_type=MESH,
        )

    for d in range(1, n_img):
        to_img(mass_buf, mass_buf, d, ms_sem, mr_sem).start()

    def numer(target, store):
        def step(c, carry):
            at = pl.multiple_of(target * part_freq + c * chunk, LANES)
            at_im = pl.multiple_of(freq + target * part_freq + c * chunk, LANES)
            low = rho_low[...]
            sum_re = jnp.dot(
                low, wbuf[:, :, pl.ds(at, chunk)].reshape(total, chunk),
                preferred_element_type=jnp.float32,
            )
            sum_im = jnp.dot(
                low, wbuf[:, :, pl.ds(at_im, chunk)].reshape(total, chunk),
                preferred_element_type=jnp.float32,
            )
            acc_re = jnp.zeros((classes, chunk), jnp.float32)
            acc_im = jnp.zeros((classes, chunk), jnp.float32)
            for r in range(poses):
                cos_r = cos_ref[r : r + 1, pl.ds(at, chunk)]
                sin_r = sin_ref[r : r + 1, pl.ds(at, chunk)]
                s_re = sum_re[r * classes : (r + 1) * classes]
                s_im = sum_im[r * classes : (r + 1) * classes]
                acc_re += s_re * cos_r + s_im * sin_r
                acc_im += s_im * cos_r - s_re * sin_r
            store(pl.multiple_of(c * chunk, LANES), acc_re, acc_im)
            return carry

        lax.fori_loop(0, part_freq // chunk, step, 0)

    for d in range(1, n_img):
        def store_peer(at, re, im, d=d):
            send_buf[d, :classes, pl.ds(at, chunk)] = re.astype(send_buf.dtype)
            send_buf[d, classes:, pl.ds(at, chunk)] = im.astype(send_buf.dtype)

        numer(lax.rem(my_img + d, n_img), store_peer)
        to_img(send_buf, recv_buf, d, ns_sem, nr_sem).start()

    def store_own(at, re, im):
        own[:classes, pl.ds(at, chunk)] = re
        own[classes:, pl.ds(at, chunk)] = im

    numer(my_img, store_own)

    for d in range(1, n_img):
        to_img(mass_buf, mass_buf, d, ms_sem, mr_sem).wait_recv()
    mass = mass_buf[0]
    for d in range(1, n_img):
        mass += mass_buf[d]
    mine = pl.ds(pl.multiple_of(my_img * part_freq, LANES), part_freq)
    ctf = ctf_ref[:, mine]
    denom = jnp.dot(
        mass[:, :groups], ctf * ctf * nw_ref[:, mine], precision=HIGHEST,
        preferred_element_type=jnp.float32,
    ) + prior_precision

    for d in range(1, n_img):
        to_img(send_buf, recv_buf, d, ns_sem, nr_sem).wait_recv()
    for part in range(2):
        at = slice(part * classes, (part + 1) * classes)
        value_sum = own[at]
        for d in range(1, n_img):
            value_sum += recv_buf[d, at].astype(jnp.float32)
        avg_ref[part] = value_sum / denom

    for d in range(1, n_cls):
        stat_copy(d).wait_send()

    def drain(h, carry):
        for p in range(pieces):
            @pl.when(has_right & (my_cls - h >= 0))
            def _(p=p):
                hop(my_cls - h, p, True).wait_send()

            @pl.when(has_left & (my_cls + h < n_cls))
            def _(p=p):
                hop(my_cls + h, p, False).wait_send()
        return carry

    lax.fori_loop(0, n_cls - 1, drain, 0)
    for d in range(1, n_img):
        to_img(mass_buf, mass_buf, d, ms_sem, mr_sem).wait_send()
        to_img(send_buf, recv_buf, d, ns_sem, nr_sem).wait_send()


def local(n_cls, n_img, particles, classes, ctf, noise_weight, group_ids, shifts):
    rows, _, freq = particles.shape
    cls_rows = classes.shape[0]
    poses = shifts.shape[0]
    groups = ctf.shape[0]
    total = rows * n_cls
    part_freq = freq // n_img
    chunk = 384 if part_freq % 384 == 0 else LANES
    pad_groups = -(-groups // LANES) * LANES
    pad_total = -(-total // LANES) * LANES
    pieces = next(p for p in (4, 3, 2, 1) if 2 * freq % (p * 2 * chunk) == 0)
    vmem = pl.BlockSpec(memory_space=pltpu.VMEM)
    dma = pltpu.SemaphoreType.DMA
    resp, avg = pl.pallas_call(
        functools.partial(kernel, n_cls, n_img, chunk, pieces),
        out_shape=(
            jax.ShapeDtypeStruct((cls_rows, total), jnp.float32),
            jax.ShapeDtypeStruct((2, cls_rows, part_freq), jnp.float32),
        ),
        in_specs=[pl.BlockSpec(memory_space=pltpu.SMEM)] + [vmem] * 5,
        out_specs=(vmem, vmem),
        scratch_shapes=[
            pltpu.VMEM((n_cls, rows, 2 * freq + pad_groups), jnp.bfloat16),
            pltpu.VMEM((rows, freq), jnp.float32),
            pltpu.VMEM((rows, pad_groups), jnp.float32),
            pltpu.VMEM((poses, freq), jnp.float32),
            pltpu.VMEM((poses, freq), jnp.float32),
            pltpu.VMEM((poses * cls_rows, 2 * freq), jnp.bfloat16),
            pltpu.VMEM((poses * cls_rows, total), jnp.float32),
            pltpu.VMEM((poses * cls_rows, total), jnp.bfloat16),
            pltpu.VMEM((n_cls, 8, pad_total), jnp.float32),
            pltpu.VMEM((n_img, cls_rows, pad_groups), jnp.float32),
            pltpu.VMEM((n_img, 2 * cls_rows, part_freq), jnp.bfloat16),
            pltpu.VMEM((n_img, 2 * cls_rows, part_freq), jnp.bfloat16),
            pltpu.VMEM((2 * cls_rows, part_freq), jnp.float32),
            dma((n_cls, pieces)), dma((n_cls, pieces)), dma((n_cls, pieces)),
            dma((n_cls,)), dma((n_cls,)),
            dma((n_img,)), dma((n_img,)), dma((n_img,)), dma((n_img,)),
        ],
        compiler_params=pltpu.CompilerParams(
            collective_id=0, has_side_effects=True, vmem_limit_bytes=56 << 20
        ),
    )(
        group_ids,
        particles.reshape(rows, 2 * freq),
        classes.reshape(cls_rows, 2 * freq),
        ctf,
        noise_weight[None, :],
        shifts,
    )
    return resp.T, avg.transpose(1, 0, 2)


def solution(mesh):
    placed = (
        P(("groups", "img", "cls"), None, None),
        P(("groups", "cls"), None, None),
        P("groups", None),
        P("groups"),
        P(("groups", "img", "cls")),
        P("groups", None),
    )
    return jax.shard_map(
        functools.partial(local, mesh.shape["cls"], mesh.shape["img"]),
        mesh=mesh,
        in_specs=placed,
        out_specs=(P(("groups", "img"), "cls"), P(("groups", "cls"), None, "img")),
        check_vma=False,
    )
```

```python
import functools

import jax
import jax.numpy as jnp
from jax import lax
from jax.experimental import pallas as pl
from jax.experimental.pallas import tpu as pltpu
from jax.sharding import PartitionSpec as P

BOX = 128
LANES = 128
MESH = pl.DeviceIdType.MESH
HIGHEST = lax.Precision.HIGHEST
NT = (((1,), (1,)), ((), ()))

prior_precision = 0.02


def fill_phase_tables(shift_ref, cos_ref, sin_ref):
    poses, freq = cos_ref.shape
    step = 2.0 * jnp.pi / BOX
    lane = lax.broadcasted_iota(jnp.int32, (poses, BOX), 1)
    pose = lax.broadcasted_iota(jnp.int32, (poses, BOX), 0)
    move_x = jnp.zeros((poses, BOX), jnp.int32)
    move_y = jnp.zeros((poses, BOX), jnp.int32)
    for r in range(poses):
        move_x = jnp.where(pose == r, shift_ref[0, r], move_x)
        move_y = jnp.where(pose == r, shift_ref[1, r], move_y)
    move_x, move_y = move_x.astype(jnp.float32), move_y.astype(jnp.float32)
    angle_x = step * (move_x * (lane - BOX // 2).astype(jnp.float32))
    cos_x, sin_x = jnp.cos(angle_x), jnp.sin(angle_x)
    for row in range(freq // BOX):
        if row % BOX == 0:
            angle_y = step * (move_y * (lane + row).astype(jnp.float32))
            cos_rows, sin_rows = jnp.cos(angle_y), jnp.sin(angle_y)
        cos_y = cos_rows[:, row % BOX : row % BOX + 1]
        sin_y = sin_rows[:, row % BOX : row % BOX + 1]
        cols = slice(row * BOX, (row + 1) * BOX)
        cos_ref[:, cols] = cos_x * cos_y - sin_x * sin_y
        sin_ref[:, cols] = sin_x * cos_y + cos_x * sin_y


def kernel(
    n_cls, n_img, chunk, pieces,
    ids_s, shift_ref, part_hbm, cls_hbm, ctf_hbm, nw_hbm,
    resp_ref, avg_ref,
    part_ref, cls_ref, ctf_ref, nw_ref, wbuf, sel, onehot, cos_ref, sin_ref, temps, scores, rho_low, stat, mass_buf, send_buf, recv_buf, own,
    in_sem, right_sem, left_sem, gr_sem, ss_sem, sr_sem, ms_sem, mr_sem, ns_sem, nr_sem,
):
    rows = part_ref.shape[0]
    freq = ctf_ref.shape[1]
    groups = ctf_ref.shape[0]
    classes = cls_ref.shape[0]
    poses = cos_ref.shape[0]
    total = rows * n_cls
    part_freq = freq // n_img
    my_cls = lax.axis_index("cls")
    my_img = lax.axis_index("img")

    barrier = pltpu.get_barrier_semaphore()
    for d in range(1, n_cls):
        pl.semaphore_signal(
            barrier, inc=1, device_id={"cls": lax.rem(my_cls + d, n_cls)}, device_id_type=MESH
        )
    for d in range(1, n_img):
        pl.semaphore_signal(
            barrier, inc=1, device_id={"img": lax.rem(my_img + d, n_img)}, device_id_type=MESH
        )

    inputs = [
        pltpu.make_async_copy(src, dst, in_sem.at[i])
        for i, (src, dst) in enumerate(
            ((ctf_hbm, ctf_ref), (nw_hbm, nw_ref), (part_hbm, part_ref), (cls_hbm, cls_ref))
        )
    ]
    for copy in inputs:
        copy.start()
    for copy in inputs[:3]:
        copy.wait()

    for i in range(rows):
        sel[pl.ds(i, 1), :] = ctf_ref[pl.ds(ids_s[i], 1), :] * nw_ref[...]
        onehot[pl.ds(i, 1), :] = (
            lax.broadcasted_iota(jnp.int32, (1, onehot.shape[1]), 1) == ids_s[i]
        ).astype(jnp.float32)
    for part in range(2):
        cols = slice(part * freq, (part + 1) * freq)
        wbuf[my_cls, :, cols] = (
            part_ref[:, cols].astype(jnp.float32) * sel[...]
        ).astype(jnp.bfloat16)
    pad_groups = wbuf.shape[2] - 2 * freq
    wbuf[my_cls, :, 2 * freq :] = onehot[...].astype(jnp.bfloat16)

    pl.semaphore_wait(barrier, n_cls + n_img - 2)

    width = 2 * freq // pieces

    def hop(slot, p, to_right):
        last = pad_groups if p == pieces - 1 else 0
        cols = pl.ds(p * width, width + last)
        return pltpu.make_async_remote_copy(
            src_ref=wbuf.at[slot, :, cols],
            dst_ref=wbuf.at[slot, :, cols],
            send_sem=(right_sem if to_right else left_sem).at[slot, p],
            recv_sem=gr_sem.at[slot, p],
            device_id={"cls": my_cls + 1 if to_right else my_cls - 1},
            device_id_type=MESH,
        )

    has_right = my_cls < n_cls - 1
    has_left = my_cls > 0

    def start_right(slot, p):
        @pl.when(has_right)
        def _():
            hop(slot, p, True).start()

    def start_left(slot, p):
        @pl.when(has_left)
        def _():
            hop(slot, p, False).start()

    def relay(h, p):
        @pl.when(my_cls - h >= 0)
        def _():
            hop(my_cls - h, p, False).wait_recv()
            start_right(my_cls - h, p)

        @pl.when(my_cls + h < n_cls)
        def _():
            hop(my_cls + h, p, True).wait_recv()
            start_left(my_cls + h, p)

    for p in range(pieces):
        start_right(my_cls, p)
        start_left(my_cls, p)

    fill_phase_tables(shift_ref, cos_ref, sin_ref)

    inputs[3].wait()

    def build(c, power):
        at = pl.multiple_of(c * chunk, LANES)
        at_im = pl.multiple_of(freq + c * chunk, LANES)
        re = cls_ref[:, pl.ds(at, chunk)].astype(jnp.float32)
        im = cls_ref[:, pl.ds(at_im, chunk)].astype(jnp.float32)
        for r in range(poses):
            cos_r = cos_ref[r : r + 1, pl.ds(at, chunk)]
            sin_r = sin_ref[r : r + 1, pl.ds(at, chunk)]
            out = slice(r * classes, (r + 1) * classes)
            temps[out, pl.ds(at, chunk)] = (re * cos_r - im * sin_r).astype(jnp.bfloat16)
            temps[out, pl.ds(at_im, chunk)] = (re * sin_r + im * cos_r).astype(jnp.bfloat16)
        ctf = ctf_ref[:, pl.ds(at, chunk)]
        weight = ctf * ctf * nw_ref[:, pl.ds(at, chunk)]
        return power + lax.dot_general(
            re * re + im * im, weight, NT, precision=HIGHEST,
            preferred_element_type=jnp.float32,
        )

    power = lax.fori_loop(
        0, freq // chunk, build, jnp.zeros((classes, groups), jnp.float32)
    )

    scores[...] = jnp.zeros_like(scores)

    def relay_all(h, carry):
        for p in range(pieces):
            relay(h, p)
        return carry

    lax.fori_loop(1, n_cls - 1, relay_all, 0)

    for p in range(pieces):
        relay(n_cls - 1, p)
        cols = slice(p * width, (p + 1) * width)
        scores[...] += lax.dot_general(
            temps[:, cols],
            wbuf[:, :, cols].reshape(total, width),
            NT,
            preferred_element_type=jnp.float32,
        )

    marks = wbuf[:, :, 2 * freq :].reshape(total, pad_groups)[:, :groups].astype(jnp.float32)
    penalty = lax.dot_general(
        power, marks, NT, precision=HIGHEST, preferred_element_type=jnp.float32
    )
    value = scores[...].reshape(poses, classes, total) - 0.5 * penalty[None]
    pose_peak = jnp.max(value, axis=0)
    pose_sum = jnp.sum(jnp.exp(value - pose_peak[None]), axis=0)
    peak = jnp.max(pose_peak, axis=0, keepdims=True)
    stat[0, 0:1, :total] = peak
    stat[0, 1:2, :total] = jnp.sum(
        pose_sum * jnp.exp(pose_peak - peak), axis=0, keepdims=True
    )

    def stat_copy(d):
        return pltpu.make_async_remote_copy(
            src_ref=stat.at[0],
            dst_ref=stat.at[d],
            send_sem=ss_sem.at[d],
            recv_sem=sr_sem.at[d],
            device_id={"cls": lax.rem(my_cls + d, n_cls)},
            device_id_type=MESH,
        )

    for d in range(1, n_cls):
        stat_copy(d).start()
    for d in range(1, n_cls):
        stat_copy(d).wait_recv()
    whole_peak = peak
    for d in range(1, n_cls):
        whole_peak = jnp.maximum(whole_peak, stat[d, 0:1, :total])
    norm = jnp.zeros_like(peak)
    for d in range(n_cls):
        norm += stat[d, 1:2, :total] * jnp.exp(stat[d, 0:1, :total] - whole_peak)
    log_norm = whole_peak + jnp.log(norm)
    resp_ref[...] = pose_peak + jnp.log(pose_sum) - log_norm
    rho = jnp.exp(value - log_norm[None])
    rho_low[...] = rho.reshape(poses * classes, total).astype(jnp.bfloat16)
    mass_buf[0] = jnp.dot(
        jnp.sum(rho, axis=0),
        wbuf[:, :, 2 * freq :].reshape(total, pad_groups).astype(jnp.float32),
        precision=HIGHEST,
        preferred_element_type=jnp.float32,
    )

    def to_img(src, dst, d, send, recv):
        return pltpu.make_async_remote_copy(
            src_ref=src.at[d] if src is send_buf else src.at[0],
            dst_ref=dst.at[d],
            send_sem=send.at[d],
            recv_sem=recv.at[d],
            device_id={"img": lax.rem(my_img + d, n_img)},
            device_id_type=MESH,
        )

    for d in range(1, n_img):
        to_img(mass_buf, mass_buf, d, ms_sem, mr_sem).start()

    def numer(target, store):
        def step(c, carry):
            at = pl.multiple_of(target * part_freq + c * chunk, LANES)
            at_im = pl.multiple_of(freq + target * part_freq + c * chunk, LANES)
            low = rho_low[...]
            sum_re = jnp.dot(
                low, wbuf[:, :, pl.ds(at, chunk)].reshape(total, chunk),
                preferred_element_type=jnp.float32,
            )
            sum_im = jnp.dot(
                low, wbuf[:, :, pl.ds(at_im, chunk)].reshape(total, chunk),
                preferred_element_type=jnp.float32,
            )
            acc_re = jnp.zeros((classes, chunk), jnp.float32)
            acc_im = jnp.zeros((classes, chunk), jnp.float32)
            for r in range(poses):
                cos_r = cos_ref[r : r + 1, pl.ds(at, chunk)]
                sin_r = sin_ref[r : r + 1, pl.ds(at, chunk)]
                s_re = sum_re[r * classes : (r + 1) * classes]
                s_im = sum_im[r * classes : (r + 1) * classes]
                acc_re += s_re * cos_r + s_im * sin_r
                acc_im += s_im * cos_r - s_re * sin_r
            store(pl.multiple_of(c * chunk, LANES), acc_re, acc_im)
            return carry

        lax.fori_loop(0, part_freq // chunk, step, 0)

    def send_numer(t, carry):
        d = 1 + lax.rem(t + 1, n_img - 1)

        def store_peer(at, re, im):
            send_buf[d, :classes, pl.ds(at, chunk)] = re.astype(send_buf.dtype)
            send_buf[d, classes:, pl.ds(at, chunk)] = im.astype(send_buf.dtype)

        numer(lax.rem(my_img + d, n_img), store_peer)
        to_img(send_buf, recv_buf, d, ns_sem, nr_sem).start()
        return carry

    lax.fori_loop(0, n_img - 1, send_numer, 0)

    def store_own(at, re, im):
        own[:classes, pl.ds(at, chunk)] = re
        own[classes:, pl.ds(at, chunk)] = im

    numer(my_img, store_own)

    for d in range(1, n_img):
        to_img(mass_buf, mass_buf, d, ms_sem, mr_sem).wait_recv()
    mass = mass_buf[0]
    for d in range(1, n_img):
        mass += mass_buf[d]
    mine = pl.ds(pl.multiple_of(my_img * part_freq, LANES), part_freq)
    ctf = ctf_ref[:, mine]
    denom = jnp.dot(
        mass[:, :groups], ctf * ctf * nw_ref[:, mine], precision=HIGHEST,
        preferred_element_type=jnp.float32,
    ) + prior_precision

    for d in range(1, n_img):
        to_img(send_buf, recv_buf, d, ns_sem, nr_sem).wait_recv()
    for part in range(2):
        at = slice(part * classes, (part + 1) * classes)
        value_sum = own[at]
        for d in range(1, n_img):
            value_sum += recv_buf[d, at].astype(jnp.float32)
        avg_ref[part] = value_sum / denom

    for d in range(1, n_cls):
        stat_copy(d).wait_send()

    def drain(h, carry):
        for p in range(pieces):
            @pl.when(has_right & (my_cls - h >= 0))
            def _(p=p):
                hop(my_cls - h, p, True).wait_send()

            @pl.when(has_left & (my_cls + h < n_cls))
            def _(p=p):
                hop(my_cls + h, p, False).wait_send()
        return carry

    lax.fori_loop(0, n_cls - 1, drain, 0)
    for d in range(1, n_img):
        to_img(mass_buf, mass_buf, d, ms_sem, mr_sem).wait_send()
        to_img(send_buf, recv_buf, d, ns_sem, nr_sem).wait_send()


def local(n_cls, n_img, particles, classes, ctf, noise_weight, group_ids, shifts):
    rows, _, freq = particles.shape
    cls_rows = classes.shape[0]
    poses = shifts.shape[0]
    groups = ctf.shape[0]
    total = rows * n_cls
    part_freq = freq // n_img
    chunk = 384 if part_freq % 384 == 0 else LANES
    pad_groups = -(-groups // LANES) * LANES
    pad_total = -(-total // LANES) * LANES
    pieces = next(p for p in (4, 3, 2, 1) if 2 * freq % (p * 2 * chunk) == 0)
    vmem = pl.BlockSpec(memory_space=pltpu.VMEM)
    dma = pltpu.SemaphoreType.DMA
    resp, avg = pl.pallas_call(
        functools.partial(kernel, n_cls, n_img, chunk, pieces),
        out_shape=(
            jax.ShapeDtypeStruct((cls_rows, total), jnp.float32),
            jax.ShapeDtypeStruct((2, cls_rows, part_freq), jnp.float32),
        ),
        in_specs=[pl.BlockSpec(memory_space=pltpu.SMEM)] * 2
        + [pl.BlockSpec(memory_space=pl.ANY)] * 4,
        out_specs=(vmem, vmem),
        scratch_shapes=[
            pltpu.VMEM((rows, 2 * freq), jnp.bfloat16),
            pltpu.VMEM((cls_rows, 2 * freq), jnp.bfloat16),
            pltpu.VMEM((groups, freq), jnp.float32),
            pltpu.VMEM((1, freq), jnp.float32),
            pltpu.VMEM((n_cls, rows, 2 * freq + pad_groups), jnp.bfloat16),
            pltpu.VMEM((rows, freq), jnp.float32),
            pltpu.VMEM((rows, pad_groups), jnp.float32),
            pltpu.VMEM((poses, freq), jnp.float32),
            pltpu.VMEM((poses, freq), jnp.float32),
            pltpu.VMEM((poses * cls_rows, 2 * freq), jnp.bfloat16),
            pltpu.VMEM((poses * cls_rows, total), jnp.float32),
            pltpu.VMEM((poses * cls_rows, total), jnp.bfloat16),
            pltpu.VMEM((n_cls, 8, pad_total), jnp.float32),
            pltpu.VMEM((n_img, cls_rows, pad_groups), jnp.float32),
            pltpu.VMEM((n_img, 2 * cls_rows, part_freq), jnp.bfloat16),
            pltpu.VMEM((n_img, 2 * cls_rows, part_freq), jnp.bfloat16),
            pltpu.VMEM((2 * cls_rows, part_freq), jnp.float32),
            dma((4,)),
            dma((n_cls, pieces)), dma((n_cls, pieces)), dma((n_cls, pieces)),
            dma((n_cls,)), dma((n_cls,)),
            dma((n_img,)), dma((n_img,)), dma((n_img,)), dma((n_img,)),
        ],
        compiler_params=pltpu.CompilerParams(
            collective_id=0, has_side_effects=True, vmem_limit_bytes=56 << 20
        ),
    )(
        group_ids,
        shifts.T,
        particles.reshape(rows, 2 * freq),
        classes.reshape(cls_rows, 2 * freq),
        ctf,
        noise_weight.reshape(1, freq),
    )
    return resp.T, avg.transpose(1, 0, 2)


def solution(mesh):
    placed = (
        P(("groups", "img", "cls"), None, None),
        P(("groups", "cls"), None, None),
        P("groups", None),
        P("groups"),
        P(("groups", "img", "cls")),
        P("groups", None),
    )
    return jax.shard_map(
        functools.partial(local, mesh.shape["cls"], mesh.shape["img"]),
        mesh=mesh,
        in_specs=placed,
        out_specs=(P(("groups", "img"), "cls"), P(("groups", "cls"), None, "img")),
        check_vma=False,
    )
```

```python
import functools

import jax
import jax.numpy as jnp
from jax import lax
from jax.experimental import pallas as pl
from jax.experimental.pallas import tpu as pltpu
from jax.sharding import PartitionSpec as P

BOX = 128
LANES = 128
MESH = pl.DeviceIdType.MESH
HIGHEST = lax.Precision.HIGHEST
NT = (((1,), (1,)), ((), ()))

prior_precision = 0.02


def fill_phase_tables(shift_ref, cos_ref, sin_ref):
    poses, freq = cos_ref.shape
    step = 2.0 * jnp.pi / BOX
    lane = lax.broadcasted_iota(jnp.int32, (poses, BOX), 1)
    pose = lax.broadcasted_iota(jnp.int32, (poses, BOX), 0)
    move_x = jnp.zeros((poses, BOX), jnp.int32)
    move_y = jnp.zeros((poses, BOX), jnp.int32)
    for r in range(poses):
        move_x = jnp.where(pose == r, shift_ref[0, r], move_x)
        move_y = jnp.where(pose == r, shift_ref[1, r], move_y)
    move_x, move_y = move_x.astype(jnp.float32), move_y.astype(jnp.float32)
    angle_x = step * (move_x * (lane - BOX // 2).astype(jnp.float32))
    cos_x, sin_x = jnp.cos(angle_x), jnp.sin(angle_x)
    for row in range(freq // BOX):
        if row % BOX == 0:
            angle_y = step * (move_y * (lane + row).astype(jnp.float32))
            cos_rows, sin_rows = jnp.cos(angle_y), jnp.sin(angle_y)
        cos_y = cos_rows[:, row % BOX : row % BOX + 1]
        sin_y = sin_rows[:, row % BOX : row % BOX + 1]
        cols = slice(row * BOX, (row + 1) * BOX)
        cos_ref[:, cols] = cos_x * cos_y - sin_x * sin_y
        sin_ref[:, cols] = sin_x * cos_y + cos_x * sin_y


def kernel(
    n_cls, n_img, chunk, pieces,
    ids_s, shift_ref, part_hbm, cls_hbm, ctf_hbm, nw_hbm,
    resp_ref, avg_ref,
    part_ref, cls_ref, ctf_ref, nw_ref, wbuf, sel, onehot, cos_ref, sin_ref, temps, scores, rho_low, stat, mass_buf, send_buf, recv_buf, own,
    in_sem, right_sem, left_sem, gr_sem, ss_sem, sr_sem, ms_sem, mr_sem, ns_sem, nr_sem,
):
    rows = part_ref.shape[0]
    freq = ctf_ref.shape[1]
    groups = ctf_ref.shape[0]
    classes = cls_ref.shape[0]
    poses = cos_ref.shape[0]
    total = rows * n_cls
    part_freq = freq // n_img
    my_cls = lax.axis_index("cls")
    my_img = lax.axis_index("img")

    barrier = pltpu.get_barrier_semaphore()
    for d in range(1, n_cls):
        pl.semaphore_signal(
            barrier, inc=1, device_id={"cls": lax.rem(my_cls + d, n_cls)}, device_id_type=MESH
        )
    for d in range(1, n_img):
        pl.semaphore_signal(
            barrier, inc=1, device_id={"img": lax.rem(my_img + d, n_img)}, device_id_type=MESH
        )

    inputs = [
        pltpu.make_async_copy(src, dst, in_sem.at[i])
        for i, (src, dst) in enumerate(
            ((ctf_hbm, ctf_ref), (nw_hbm, nw_ref.at[0]), (part_hbm, part_ref), (cls_hbm, cls_ref))
        )
    ]
    for copy in inputs:
        copy.start()
    for copy in inputs[:3]:
        copy.wait()

    for i in range(rows):
        sel[pl.ds(i, 1), :] = ctf_ref[pl.ds(ids_s[i], 1), :] * nw_ref[...]
        onehot[pl.ds(i, 1), :] = (
            lax.broadcasted_iota(jnp.int32, (1, onehot.shape[1]), 1) == ids_s[i]
        ).astype(jnp.float32)
    for part in range(2):
        cols = slice(part * freq, (part + 1) * freq)
        wbuf[my_cls, :, cols] = (
            part_ref[:, part].astype(jnp.float32) * sel[...]
        ).astype(jnp.bfloat16)
    pad_groups = wbuf.shape[2] - 2 * freq
    wbuf[my_cls, :, 2 * freq :] = onehot[...].astype(jnp.bfloat16)

    pl.semaphore_wait(barrier, n_cls + n_img - 2)

    width = 2 * freq // pieces

    def hop(slot, p, to_right):
        last = pad_groups if p == pieces - 1 else 0
        cols = pl.ds(p * width, width + last)
        return pltpu.make_async_remote_copy(
            src_ref=wbuf.at[slot, :, cols],
            dst_ref=wbuf.at[slot, :, cols],
            send_sem=(right_sem if to_right else left_sem).at[slot, p],
            recv_sem=gr_sem.at[slot, p],
            device_id={"cls": my_cls + 1 if to_right else my_cls - 1},
            device_id_type=MESH,
        )

    has_right = my_cls < n_cls - 1
    has_left = my_cls > 0

    def start_right(slot, p):
        @pl.when(has_right)
        def _():
            hop(slot, p, True).start()

    def start_left(slot, p):
        @pl.when(has_left)
        def _():
            hop(slot, p, False).start()

    def relay(h, p):
        @pl.when(my_cls - h >= 0)
        def _():
            hop(my_cls - h, p, False).wait_recv()
            start_right(my_cls - h, p)

        @pl.when(my_cls + h < n_cls)
        def _():
            hop(my_cls + h, p, True).wait_recv()
            start_left(my_cls + h, p)

    for p in range(pieces):
        start_right(my_cls, p)
        start_left(my_cls, p)

    fill_phase_tables(shift_ref, cos_ref, sin_ref)

    inputs[3].wait()

    def build(c, power):
        at = pl.multiple_of(c * chunk, LANES)
        at_im = pl.multiple_of(freq + c * chunk, LANES)
        re = cls_ref[:, 0, pl.ds(at, chunk)].astype(jnp.float32)
        im = cls_ref[:, 1, pl.ds(at, chunk)].astype(jnp.float32)
        for r in range(poses):
            cos_r = cos_ref[r : r + 1, pl.ds(at, chunk)]
            sin_r = sin_ref[r : r + 1, pl.ds(at, chunk)]
            out = slice(r * classes, (r + 1) * classes)
            temps[out, pl.ds(at, chunk)] = (re * cos_r - im * sin_r).astype(jnp.bfloat16)
            temps[out, pl.ds(at_im, chunk)] = (re * sin_r + im * cos_r).astype(jnp.bfloat16)
        ctf = ctf_ref[:, pl.ds(at, chunk)]
        weight = ctf * ctf * nw_ref[:, pl.ds(at, chunk)]
        return power + lax.dot_general(
            re * re + im * im, weight, NT, precision=HIGHEST,
            preferred_element_type=jnp.float32,
        )

    power = lax.fori_loop(
        0, freq // chunk, build, jnp.zeros((classes, groups), jnp.float32)
    )

    scores[...] = jnp.zeros_like(scores)

    def relay_all(h, carry):
        for p in range(pieces):
            relay(h, p)
        return carry

    lax.fori_loop(1, n_cls - 1, relay_all, 0)

    for p in range(pieces):
        relay(n_cls - 1, p)
        cols = slice(p * width, (p + 1) * width)
        scores[...] += lax.dot_general(
            temps[:, cols],
            wbuf[:, :, cols].reshape(total, width),
            NT,
            preferred_element_type=jnp.float32,
        )

    marks = wbuf[:, :, 2 * freq :].reshape(total, pad_groups)[:, :groups].astype(jnp.float32)
    penalty = lax.dot_general(
        power, marks, NT, precision=HIGHEST, preferred_element_type=jnp.float32
    )
    value = scores[...].reshape(poses, classes, total) - 0.5 * penalty[None]
    pose_peak = jnp.max(value, axis=0)
    pose_sum = jnp.sum(jnp.exp(value - pose_peak[None]), axis=0)
    peak = jnp.max(pose_peak, axis=0, keepdims=True)
    stat[0, 0:1, :total] = peak
    stat[0, 1:2, :total] = jnp.sum(
        pose_sum * jnp.exp(pose_peak - peak), axis=0, keepdims=True
    )

    def stat_copy(d):
        return pltpu.make_async_remote_copy(
            src_ref=stat.at[0],
            dst_ref=stat.at[d],
            send_sem=ss_sem.at[d],
            recv_sem=sr_sem.at[d],
            device_id={"cls": lax.rem(my_cls + d, n_cls)},
            device_id_type=MESH,
        )

    for d in range(1, n_cls):
        stat_copy(d).start()
    for d in range(1, n_cls):
        stat_copy(d).wait_recv()
    whole_peak = peak
    for d in range(1, n_cls):
        whole_peak = jnp.maximum(whole_peak, stat[d, 0:1, :total])
    norm = jnp.zeros_like(peak)
    for d in range(n_cls):
        norm += stat[d, 1:2, :total] * jnp.exp(stat[d, 0:1, :total] - whole_peak)
    log_norm = whole_peak + jnp.log(norm)
    resp_ref[...] = pose_peak + jnp.log(pose_sum) - log_norm
    rho = jnp.exp(value - log_norm[None])
    rho_low[...] = rho.reshape(poses * classes, total).astype(jnp.bfloat16)
    mass_buf[0] = jnp.dot(
        jnp.sum(rho, axis=0),
        wbuf[:, :, 2 * freq :].reshape(total, pad_groups).astype(jnp.float32),
        precision=HIGHEST,
        preferred_element_type=jnp.float32,
    )

    def to_img(src, dst, d, send, recv):
        return pltpu.make_async_remote_copy(
            src_ref=src.at[d] if src is send_buf else src.at[0],
            dst_ref=dst.at[d],
            send_sem=send.at[d],
            recv_sem=recv.at[d],
            device_id={"img": lax.rem(my_img + d, n_img)},
            device_id_type=MESH,
        )

    for d in range(1, n_img):
        to_img(mass_buf, mass_buf, d, ms_sem, mr_sem).start()

    def numer(target, store):
        def step(c, carry):
            at = pl.multiple_of(target * part_freq + c * chunk, LANES)
            at_im = pl.multiple_of(freq + target * part_freq + c * chunk, LANES)
            low = rho_low[...]
            sum_re = jnp.dot(
                low, wbuf[:, :, pl.ds(at, chunk)].reshape(total, chunk),
                preferred_element_type=jnp.float32,
            )
            sum_im = jnp.dot(
                low, wbuf[:, :, pl.ds(at_im, chunk)].reshape(total, chunk),
                preferred_element_type=jnp.float32,
            )
            acc_re = jnp.zeros((classes, chunk), jnp.float32)
            acc_im = jnp.zeros((classes, chunk), jnp.float32)
            for r in range(poses):
                cos_r = cos_ref[r : r + 1, pl.ds(at, chunk)]
                sin_r = sin_ref[r : r + 1, pl.ds(at, chunk)]
                s_re = sum_re[r * classes : (r + 1) * classes]
                s_im = sum_im[r * classes : (r + 1) * classes]
                acc_re += s_re * cos_r + s_im * sin_r
                acc_im += s_im * cos_r - s_re * sin_r
            store(pl.multiple_of(c * chunk, LANES), acc_re, acc_im)
            return carry

        lax.fori_loop(0, part_freq // chunk, step, 0)

    def send_numer(t, carry):
        d = 1 + lax.rem(t + 1, n_img - 1)

        def store_peer(at, re, im):
            send_buf[d, :classes, pl.ds(at, chunk)] = re.astype(send_buf.dtype)
            send_buf[d, classes:, pl.ds(at, chunk)] = im.astype(send_buf.dtype)

        numer(lax.rem(my_img + d, n_img), store_peer)
        to_img(send_buf, recv_buf, d, ns_sem, nr_sem).start()
        return carry

    lax.fori_loop(0, n_img - 1, send_numer, 0)

    def store_own(at, re, im):
        own[:classes, pl.ds(at, chunk)] = re
        own[classes:, pl.ds(at, chunk)] = im

    numer(my_img, store_own)

    for d in range(1, n_img):
        to_img(mass_buf, mass_buf, d, ms_sem, mr_sem).wait_recv()
    mass = mass_buf[0]
    for d in range(1, n_img):
        mass += mass_buf[d]
    mine = pl.ds(pl.multiple_of(my_img * part_freq, LANES), part_freq)
    ctf = ctf_ref[:, mine]
    denom = jnp.dot(
        mass[:, :groups], ctf * ctf * nw_ref[:, mine], precision=HIGHEST,
        preferred_element_type=jnp.float32,
    ) + prior_precision

    for d in range(1, n_img):
        to_img(send_buf, recv_buf, d, ns_sem, nr_sem).wait_recv()
    for part in range(2):
        at = slice(part * classes, (part + 1) * classes)
        value_sum = own[at]
        for d in range(1, n_img):
            value_sum += recv_buf[d, at].astype(jnp.float32)
        avg_ref[:, part] = value_sum / denom

    for d in range(1, n_cls):
        stat_copy(d).wait_send()

    def drain(h, carry):
        for p in range(pieces):
            @pl.when(has_right & (my_cls - h >= 0))
            def _(p=p):
                hop(my_cls - h, p, True).wait_send()

            @pl.when(has_left & (my_cls + h < n_cls))
            def _(p=p):
                hop(my_cls + h, p, False).wait_send()
        return carry

    lax.fori_loop(0, n_cls - 1, drain, 0)
    for d in range(1, n_img):
        to_img(mass_buf, mass_buf, d, ms_sem, mr_sem).wait_send()
        to_img(send_buf, recv_buf, d, ns_sem, nr_sem).wait_send()


def local(n_cls, n_img, particles, classes, ctf, noise_weight, group_ids, shifts):
    rows, _, freq = particles.shape
    cls_rows = classes.shape[0]
    poses = shifts.shape[0]
    groups = ctf.shape[0]
    total = rows * n_cls
    part_freq = freq // n_img
    chunk = 384 if part_freq % 384 == 0 else LANES
    pad_groups = -(-groups // LANES) * LANES
    pad_total = -(-total // LANES) * LANES
    pieces = next(p for p in (4, 3, 2, 1) if 2 * freq % (p * 2 * chunk) == 0)
    vmem = pl.BlockSpec(memory_space=pltpu.VMEM)
    dma = pltpu.SemaphoreType.DMA
    resp, avg = pl.pallas_call(
        functools.partial(kernel, n_cls, n_img, chunk, pieces),
        out_shape=(
            jax.ShapeDtypeStruct((cls_rows, total), jnp.float32),
            jax.ShapeDtypeStruct((cls_rows, 2, part_freq), jnp.float32),
        ),
        in_specs=[pl.BlockSpec(memory_space=pltpu.SMEM)] * 2
        + [pl.BlockSpec(memory_space=pl.ANY)] * 4,
        out_specs=(vmem, vmem),
        scratch_shapes=[
            pltpu.VMEM((rows, 2, freq), jnp.bfloat16),
            pltpu.VMEM((cls_rows, 2, freq), jnp.bfloat16),
            pltpu.VMEM((groups, freq), jnp.float32),
            pltpu.VMEM((1, freq), jnp.float32),
            pltpu.VMEM((n_cls, rows, 2 * freq + pad_groups), jnp.bfloat16),
            pltpu.VMEM((rows, freq), jnp.float32),
            pltpu.VMEM((rows, pad_groups), jnp.float32),
            pltpu.VMEM((poses, freq), jnp.float32),
            pltpu.VMEM((poses, freq), jnp.float32),
            pltpu.VMEM((poses * cls_rows, 2 * freq), jnp.bfloat16),
            pltpu.VMEM((poses * cls_rows, total), jnp.float32),
            pltpu.VMEM((poses * cls_rows, total), jnp.bfloat16),
            pltpu.VMEM((n_cls, 8, pad_total), jnp.float32),
            pltpu.VMEM((n_img, cls_rows, pad_groups), jnp.float32),
            pltpu.VMEM((n_img, 2 * cls_rows, part_freq), jnp.bfloat16),
            pltpu.VMEM((n_img, 2 * cls_rows, part_freq), jnp.bfloat16),
            pltpu.VMEM((2 * cls_rows, part_freq), jnp.float32),
            dma((4,)),
            dma((n_cls, pieces)), dma((n_cls, pieces)), dma((n_cls, pieces)),
            dma((n_cls,)), dma((n_cls,)),
            dma((n_img,)), dma((n_img,)), dma((n_img,)), dma((n_img,)),
        ],
        compiler_params=pltpu.CompilerParams(
            collective_id=0, has_side_effects=True, vmem_limit_bytes=56 << 20
        ),
    )(
        group_ids,
        shifts.T,
        particles,
        classes,
        ctf,
        noise_weight,
    )
    return resp.T, avg


def solution(mesh):
    placed = (
        P(("groups", "img", "cls"), None, None),
        P(("groups", "cls"), None, None),
        P("groups", None),
        P("groups"),
        P(("groups", "img", "cls")),
        P("groups", None),
    )
    return jax.shard_map(
        functools.partial(local, mesh.shape["cls"], mesh.shape["img"]),
        mesh=mesh,
        in_specs=placed,
        out_specs=(P(("groups", "img"), "cls"), P(("groups", "cls"), None, "img")),
        check_vma=False,
    )
```

```python
import functools

import jax
import jax.numpy as jnp
from jax import lax
from jax.experimental import pallas as pl
from jax.experimental.pallas import tpu as pltpu
from jax.sharding import PartitionSpec as P

BOX = 128
LANES = 128
MESH = pl.DeviceIdType.MESH
HIGHEST = lax.Precision.HIGHEST
NT = (((1,), (1,)), ((), ()))

prior_precision = 0.02


def fill_phase_tables(shift_ref, cos_ref, sin_ref):
    poses, freq = cos_ref.shape
    step = 2.0 * jnp.pi / BOX
    lane = lax.broadcasted_iota(jnp.int32, (poses, BOX), 1)
    pose = lax.broadcasted_iota(jnp.int32, (poses, BOX), 0)
    move_x = jnp.zeros((poses, BOX), jnp.int32)
    move_y = jnp.zeros((poses, BOX), jnp.int32)
    for r in range(poses):
        move_x = jnp.where(pose == r, shift_ref[0, r], move_x)
        move_y = jnp.where(pose == r, shift_ref[1, r], move_y)
    move_x, move_y = move_x.astype(jnp.float32), move_y.astype(jnp.float32)
    angle_x = step * (move_x * (lane - BOX // 2).astype(jnp.float32))
    cos_x, sin_x = jnp.cos(angle_x), jnp.sin(angle_x)
    for row in range(freq // BOX):
        if row % BOX == 0:
            angle_y = step * (move_y * (lane + row).astype(jnp.float32))
            cos_rows, sin_rows = jnp.cos(angle_y), jnp.sin(angle_y)
        cos_y = cos_rows[:, row % BOX : row % BOX + 1]
        sin_y = sin_rows[:, row % BOX : row % BOX + 1]
        cols = slice(row * BOX, (row + 1) * BOX)
        cos_ref[:, cols] = cos_x * cos_y - sin_x * sin_y
        sin_ref[:, cols] = sin_x * cos_y + cos_x * sin_y


def kernel(
    n_cls, n_img, chunk, pieces,
    ids_s, shift_ref, part_hbm, cls_hbm, ctf_hbm, nw_hbm,
    resp_ref, avg_ref,
    part_ref, cls_ref, ctf_ref, nw_ref, wbuf, sel, onehot, cos_ref, sin_ref, temps, scores, rho_low, stat, mass_buf, send_buf, recv_buf, own,
    in_sem, right_sem, left_sem, gr_sem, ss_sem, sr_sem, ms_sem, mr_sem, ns_sem, nr_sem,
):
    rows = part_ref.shape[0]
    freq = ctf_ref.shape[1]
    groups = ctf_ref.shape[0]
    classes = cls_ref.shape[0]
    poses = cos_ref.shape[0]
    total = rows * n_cls
    part_freq = freq // n_img
    my_cls = lax.axis_index("cls")
    my_img = lax.axis_index("img")

    barrier = pltpu.get_barrier_semaphore()
    for d in range(1, n_cls):
        pl.semaphore_signal(
            barrier, inc=1, device_id={"cls": lax.rem(my_cls + d, n_cls)}, device_id_type=MESH
        )
    for d in range(1, n_img):
        pl.semaphore_signal(
            barrier, inc=1, device_id={"img": lax.rem(my_img + d, n_img)}, device_id_type=MESH
        )

    inputs = [
        pltpu.make_async_copy(src, dst, in_sem.at[i])
        for i, (src, dst) in enumerate(
            ((ctf_hbm, ctf_ref), (nw_hbm, nw_ref.at[0]), (part_hbm, part_ref), (cls_hbm, cls_ref))
        )
    ]
    for copy in inputs:
        copy.start()
    for copy in inputs[:3]:
        copy.wait()

    for i in range(rows):
        sel[pl.ds(i, 1), :] = ctf_ref[pl.ds(ids_s[i], 1), :] * nw_ref[...]
        onehot[pl.ds(i, 1), :] = (
            lax.broadcasted_iota(jnp.int32, (1, onehot.shape[1]), 1) == ids_s[i]
        ).astype(jnp.float32)
    for part in range(2):
        cols = slice(part * freq, (part + 1) * freq)
        wbuf[my_cls, :, cols] = (
            part_ref[:, part].astype(jnp.float32) * sel[...]
        ).astype(jnp.bfloat16)
    pad_groups = wbuf.shape[2] - 2 * freq
    wbuf[my_cls, :, 2 * freq :] = onehot[...].astype(jnp.bfloat16)

    pl.semaphore_wait(barrier, n_cls + n_img - 2)

    width = 2 * freq // pieces

    def hop(slot, p, to_right):
        last = pad_groups if p == pieces - 1 else 0
        cols = pl.ds(p * width, width + last)
        return pltpu.make_async_remote_copy(
            src_ref=wbuf.at[slot, :, cols],
            dst_ref=wbuf.at[slot, :, cols],
            send_sem=(right_sem if to_right else left_sem).at[slot, p],
            recv_sem=gr_sem.at[slot, p],
            device_id={"cls": my_cls + 1 if to_right else my_cls - 1},
            device_id_type=MESH,
        )

    has_right = my_cls < n_cls - 1
    has_left = my_cls > 0

    def start_right(slot, p):
        @pl.when(has_right)
        def _():
            hop(slot, p, True).start()

    def start_left(slot, p):
        @pl.when(has_left)
        def _():
            hop(slot, p, False).start()

    def relay(h, p):
        @pl.when(my_cls - h >= 0)
        def _():
            hop(my_cls - h, p, False).wait_recv()
            start_right(my_cls - h, p)

        @pl.when(my_cls + h < n_cls)
        def _():
            hop(my_cls + h, p, True).wait_recv()
            start_left(my_cls + h, p)

    for p in range(pieces):
        start_right(my_cls, p)
        start_left(my_cls, p)

    fill_phase_tables(shift_ref, cos_ref, sin_ref)

    inputs[3].wait()

    def build(c, power):
        at = pl.multiple_of(c * chunk, LANES)
        at_im = pl.multiple_of(freq + c * chunk, LANES)
        re = cls_ref[:, 0, pl.ds(at, chunk)].astype(jnp.float32)
        im = cls_ref[:, 1, pl.ds(at, chunk)].astype(jnp.float32)
        for r in range(poses):
            cos_r = cos_ref[r : r + 1, pl.ds(at, chunk)]
            sin_r = sin_ref[r : r + 1, pl.ds(at, chunk)]
            out = slice(r * classes, (r + 1) * classes)
            temps[out, pl.ds(at, chunk)] = (re * cos_r - im * sin_r).astype(jnp.bfloat16)
            temps[out, pl.ds(at_im, chunk)] = (re * sin_r + im * cos_r).astype(jnp.bfloat16)
        ctf = ctf_ref[:, pl.ds(at, chunk)]
        weight = ctf * ctf * nw_ref[:, pl.ds(at, chunk)]
        return power + lax.dot_general(
            re * re + im * im, weight, NT, precision=HIGHEST,
            preferred_element_type=jnp.float32,
        )

    def relay_all(h, carry):
        for p in range(pieces):
            relay(h, p)
        return carry

    steps = freq // chunk
    early = steps * 2 // 3
    power = lax.fori_loop(0, early, build, jnp.zeros((classes, groups), jnp.float32))
    if n_cls > 2:
        relay_all(1, 0)
    power = lax.fori_loop(early, steps, build, power)
    scores[...] = jnp.zeros_like(scores)
    lax.fori_loop(2, n_cls - 1, relay_all, 0)

    for p in range(pieces):
        relay(n_cls - 1, p)
        cols = slice(p * width, (p + 1) * width)
        scores[...] += lax.dot_general(
            temps[:, cols],
            wbuf[:, :, cols].reshape(total, width),
            NT,
            preferred_element_type=jnp.float32,
        )

    marks = wbuf[:, :, 2 * freq :].reshape(total, pad_groups)[:, :groups].astype(jnp.float32)
    penalty = lax.dot_general(
        power, marks, NT, precision=HIGHEST, preferred_element_type=jnp.float32
    )
    value = scores[...].reshape(poses, classes, total) - 0.5 * penalty[None]
    pose_peak = jnp.max(value, axis=0)
    pose_sum = jnp.sum(jnp.exp(value - pose_peak[None]), axis=0)
    peak = jnp.max(pose_peak, axis=0, keepdims=True)
    stat[0, 0:1, :total] = peak
    stat[0, 1:2, :total] = jnp.sum(
        pose_sum * jnp.exp(pose_peak - peak), axis=0, keepdims=True
    )

    def stat_copy(d):
        return pltpu.make_async_remote_copy(
            src_ref=stat.at[0],
            dst_ref=stat.at[d],
            send_sem=ss_sem.at[d],
            recv_sem=sr_sem.at[d],
            device_id={"cls": lax.rem(my_cls + d, n_cls)},
            device_id_type=MESH,
        )

    for d in range(1, n_cls):
        stat_copy(d).start()
    for d in range(1, n_cls):
        stat_copy(d).wait_recv()
    whole_peak = peak
    for d in range(1, n_cls):
        whole_peak = jnp.maximum(whole_peak, stat[d, 0:1, :total])
    norm = jnp.zeros_like(peak)
    for d in range(n_cls):
        norm += stat[d, 1:2, :total] * jnp.exp(stat[d, 0:1, :total] - whole_peak)
    log_norm = whole_peak + jnp.log(norm)
    resp_ref[...] = pose_peak + jnp.log(pose_sum) - log_norm
    rho = jnp.exp(value - log_norm[None])
    rho_low[...] = rho.reshape(poses * classes, total).astype(jnp.bfloat16)
    mass_buf[0] = jnp.dot(
        jnp.sum(rho, axis=0),
        wbuf[:, :, 2 * freq :].reshape(total, pad_groups).astype(jnp.float32),
        precision=HIGHEST,
        preferred_element_type=jnp.float32,
    )

    def to_img(src, dst, d, send, recv):
        return pltpu.make_async_remote_copy(
            src_ref=src.at[d] if src is send_buf else src.at[0],
            dst_ref=dst.at[d],
            send_sem=send.at[d],
            recv_sem=recv.at[d],
            device_id={"img": lax.rem(my_img + d, n_img)},
            device_id_type=MESH,
        )

    for d in range(1, n_img):
        to_img(mass_buf, mass_buf, d, ms_sem, mr_sem).start()

    def numer(target, store):
        def step(c, carry):
            at = pl.multiple_of(target * part_freq + c * chunk, LANES)
            at_im = pl.multiple_of(freq + target * part_freq + c * chunk, LANES)
            low = rho_low[...]
            sum_re = jnp.dot(
                low, wbuf[:, :, pl.ds(at, chunk)].reshape(total, chunk),
                preferred_element_type=jnp.float32,
            )
            sum_im = jnp.dot(
                low, wbuf[:, :, pl.ds(at_im, chunk)].reshape(total, chunk),
                preferred_element_type=jnp.float32,
            )
            acc_re = jnp.zeros((classes, chunk), jnp.float32)
            acc_im = jnp.zeros((classes, chunk), jnp.float32)
            for r in range(poses):
                cos_r = cos_ref[r : r + 1, pl.ds(at, chunk)]
                sin_r = sin_ref[r : r + 1, pl.ds(at, chunk)]
                s_re = sum_re[r * classes : (r + 1) * classes]
                s_im = sum_im[r * classes : (r + 1) * classes]
                acc_re += s_re * cos_r + s_im * sin_r
                acc_im += s_im * cos_r - s_re * sin_r
            store(pl.multiple_of(c * chunk, LANES), acc_re, acc_im)
            return carry

        lax.fori_loop(0, part_freq // chunk, step, 0)

    def send_numer(t, carry):
        d = 1 + lax.rem(t + 1, n_img - 1)

        def store_peer(at, re, im):
            send_buf[d, :classes, pl.ds(at, chunk)] = re.astype(send_buf.dtype)
            send_buf[d, classes:, pl.ds(at, chunk)] = im.astype(send_buf.dtype)

        numer(lax.rem(my_img + d, n_img), store_peer)
        to_img(send_buf, recv_buf, d, ns_sem, nr_sem).start()
        return carry

    lax.fori_loop(0, n_img - 1, send_numer, 0)

    def store_own(at, re, im):
        own[:classes, pl.ds(at, chunk)] = re
        own[classes:, pl.ds(at, chunk)] = im

    numer(my_img, store_own)

    for d in range(1, n_img):
        to_img(mass_buf, mass_buf, d, ms_sem, mr_sem).wait_recv()
    mass = mass_buf[0]
    for d in range(1, n_img):
        mass += mass_buf[d]
    mine = pl.ds(pl.multiple_of(my_img * part_freq, LANES), part_freq)
    ctf = ctf_ref[:, mine]
    denom = jnp.dot(
        mass[:, :groups], ctf * ctf * nw_ref[:, mine], precision=HIGHEST,
        preferred_element_type=jnp.float32,
    ) + prior_precision

    for d in range(1, n_img):
        to_img(send_buf, recv_buf, d, ns_sem, nr_sem).wait_recv()
    for part in range(2):
        at = slice(part * classes, (part + 1) * classes)
        value_sum = own[at]
        for d in range(1, n_img):
            value_sum += recv_buf[d, at].astype(jnp.float32)
        avg_ref[:, part] = value_sum / denom

    for d in range(1, n_cls):
        stat_copy(d).wait_send()

    def drain(h, carry):
        for p in range(pieces):
            @pl.when(has_right & (my_cls - h >= 0))
            def _(p=p):
                hop(my_cls - h, p, True).wait_send()

            @pl.when(has_left & (my_cls + h < n_cls))
            def _(p=p):
                hop(my_cls + h, p, False).wait_send()
        return carry

    lax.fori_loop(0, n_cls - 1, drain, 0)
    for d in range(1, n_img):
        to_img(mass_buf, mass_buf, d, ms_sem, mr_sem).wait_send()
        to_img(send_buf, recv_buf, d, ns_sem, nr_sem).wait_send()


def local(n_cls, n_img, particles, classes, ctf, noise_weight, group_ids, shifts):
    rows, _, freq = particles.shape
    cls_rows = classes.shape[0]
    poses = shifts.shape[0]
    groups = ctf.shape[0]
    total = rows * n_cls
    part_freq = freq // n_img
    chunk = 384 if part_freq % 384 == 0 else LANES
    pad_groups = -(-groups // LANES) * LANES
    pad_total = -(-total // LANES) * LANES
    pieces = next(p for p in (4, 3, 2, 1) if 2 * freq % (p * 2 * chunk) == 0)
    vmem = pl.BlockSpec(memory_space=pltpu.VMEM)
    dma = pltpu.SemaphoreType.DMA
    resp, avg = pl.pallas_call(
        functools.partial(kernel, n_cls, n_img, chunk, pieces),
        out_shape=(
            jax.ShapeDtypeStruct((cls_rows, total), jnp.float32),
            jax.ShapeDtypeStruct((cls_rows, 2, part_freq), jnp.float32),
        ),
        in_specs=[pl.BlockSpec(memory_space=pltpu.SMEM)] * 2
        + [pl.BlockSpec(memory_space=pl.ANY)] * 4,
        out_specs=(vmem, vmem),
        scratch_shapes=[
            pltpu.VMEM((rows, 2, freq), jnp.bfloat16),
            pltpu.VMEM((cls_rows, 2, freq), jnp.bfloat16),
            pltpu.VMEM((groups, freq), jnp.float32),
            pltpu.VMEM((1, freq), jnp.float32),
            pltpu.VMEM((n_cls, rows, 2 * freq + pad_groups), jnp.bfloat16),
            pltpu.VMEM((rows, freq), jnp.float32),
            pltpu.VMEM((rows, pad_groups), jnp.float32),
            pltpu.VMEM((poses, freq), jnp.float32),
            pltpu.VMEM((poses, freq), jnp.float32),
            pltpu.VMEM((poses * cls_rows, 2 * freq), jnp.bfloat16),
            pltpu.VMEM((poses * cls_rows, total), jnp.float32),
            pltpu.VMEM((poses * cls_rows, total), jnp.bfloat16),
            pltpu.VMEM((n_cls, 8, pad_total), jnp.float32),
            pltpu.VMEM((n_img, cls_rows, pad_groups), jnp.float32),
            pltpu.VMEM((n_img, 2 * cls_rows, part_freq), jnp.bfloat16),
            pltpu.VMEM((n_img, 2 * cls_rows, part_freq), jnp.bfloat16),
            pltpu.VMEM((2 * cls_rows, part_freq), jnp.float32),
            dma((4,)),
            dma((n_cls, pieces)), dma((n_cls, pieces)), dma((n_cls, pieces)),
            dma((n_cls,)), dma((n_cls,)),
            dma((n_img,)), dma((n_img,)), dma((n_img,)), dma((n_img,)),
        ],
        compiler_params=pltpu.CompilerParams(
            collective_id=0, has_side_effects=True, vmem_limit_bytes=56 << 20
        ),
    )(
        group_ids,
        shifts.T,
        particles,
        classes,
        ctf,
        noise_weight,
    )
    return resp.T, avg


def solution(mesh):
    placed = (
        P(("groups", "img", "cls"), None, None),
        P(("groups", "cls"), None, None),
        P("groups", None),
        P("groups"),
        P(("groups", "img", "cls")),
        P("groups", None),
    )
    return jax.shard_map(
        functools.partial(local, mesh.shape["cls"], mesh.shape["img"]),
        mesh=mesh,
        in_specs=placed,
        out_specs=(P(("groups", "img"), "cls"), P(("groups", "cls"), None, "img")),
        check_vma=False,
    )
```
